256 devices in a mesh: chan: 8 (over x, core), ctx: 32 (over z, y).
Axes of the slice: x: 4, y: 4, z: 8, core: 2. Of those that a mesh axis runs over, the one named last changes fastest.
Arguments:
- queries: bfloat16 [4096, 8192], P('ctx', 'chan'), may hold values from -6 to 6
- keys: bfloat16 [4096, 8192], P('ctx', 'chan'), may hold values from -6 to 6
- values: bfloat16 [4096, 8192], P('ctx', 'chan'), may hold values from -6 to 6
- filters: bfloat16 [4, 4096], P(None, 'ctx'), may hold values from -0.09375 to 0.09375
- cotangent: bfloat16 [4096, 8192], P('ctx', 'chan'), may hold values from -6 to 6
Outputs:
- output: bfloat16 [4096, 8192], P('ctx', 'chan')
- query_grad: bfloat16 [4096, 8192], P('ctx', 'chan')
- key_grad: bfloat16 [4096, 8192], P('ctx', 'chan')
- value_grad: bfloat16 [4096, 8192], P('ctx', 'chan')
- filter_grad: float32 [4, 4096], P(None, 'ctx')
The draws below stay inside these ranges and needn't reach their ends.
All inputs are finite; a program needn't handle non-finite values.
Results may differ from the reference program's by a relative error of at most 0.015.
Values may be sent and summed in bfloat16 or wider, within the bound.
A program may use at most 64 MiB of HBM per device.

```python
import jax
import jax.numpy as jnp
from jax import lax

D = 8192
NFILT = 4
TOKENS = 4096


def levels(key, dims, pieces, least, top_value):
    factor_of, own = 1.0, jax.random.fold_in(key, 6)
    for dim, parts in pieces:
        draws = jnp.exp(jax.random.uniform(jax.random.fold_in(own, dim), (parts,), jnp.float32, least / len(pieces), top_value / len(pieces)))
        factor_of = factor_of * jnp.repeat(draws, dims[dim] // parts).reshape([-1 if axis == dim else 1 for axis in range(len(dims))])
    return factor_of


def centred(stream_key, extent, spread, reach, cuts=(), kind=jnp.bfloat16):
    result = spread * jax.random.normal(stream_key, extent, jnp.float32)
    if cuts:
        result = result * levels(stream_key, extent, cuts, -0.22, 0.18)
    return jnp.clip(result, -reach, reach).astype(kind)


def setup_inputs(seed: int = 0) -> dict:
    streams_of = jax.random.split(jax.random.key(seed), 6)
    queries = centred(streams_of[0], (TOKENS, D), 1.0, 6.0, ((0, 32), (1, 8)))
    keys = centred(streams_of[1], (TOKENS, D), 1.0, 6.0, ((0, 32), (1, 8)))
    values = centred(streams_of[2], (TOKENS, D), 1.0, 6.0, ((0, 32), (1, 8)))
    filters = centred(streams_of[3], (NFILT, TOKENS), TOKENS ** -0.5, 0.09375, ((1, 32),))
    cotangent = centred(streams_of[4], (TOKENS, D), 1.0, 6.0, ((0, 32), (1, 8)))
    return {"queries": queries, "keys": keys, "values": values, "filters": filters, "cotangent": cotangent}


def reference(queries, keys, values, filters, cotangent):
    tokens, width = queries.shape
    nfil = filters.shape[0]
    gated = (keys.astype(jnp.float32) * values.astype(jnp.float32)).astype(jnp.bfloat16)
    back = (cotangent.astype(jnp.float32) * queries.astype(jnp.float32)).astype(jnp.bfloat16)
    gated_cols = gated.reshape(tokens, width // nfil, nfil)
    back_cols = back.reshape(tokens, width // nfil, nfil)
    steps = jnp.arange(tokens, dtype=jnp.int32)
    lagged = steps[:, None] - steps[None, :]

    def per_filter(index):
        taps_row = lax.dynamic_index_in_dim(filters, index, 0, keepdims=False)
        picked = taps_row[jnp.clip(lagged, 0, tokens - 1)]
        toeplitz = jnp.where(lagged >= 0, picked, jnp.zeros_like(picked))
        gated_f = lax.dynamic_index_in_dim(gated_cols, index, 2, keepdims=False)
        back_f = lax.dynamic_index_in_dim(back_cols, index, 2, keepdims=False)
        mixed_f = jnp.dot(toeplitz, gated_f, preferred_element_type=jnp.float32)
        grad_f = jnp.dot(toeplitz.T, back_f, preferred_element_type=jnp.float32)
        product = jnp.dot(back_f, gated_f.T, preferred_element_type=jnp.float32)
        flipped = product[:, ::-1]
        padded = jnp.pad(flipped, ((0, 0), (0, tokens)))
        flat = padded.reshape(tokens * 2 * tokens)[: tokens * (2 * tokens - 1)]
        sums = jnp.sum(flat.reshape(tokens, 2 * tokens - 1), axis=0)
        return mixed_f, grad_f, sums[tokens - 1:]

    mixed_all, grad_all, lag_all = lax.map(per_filter, jnp.arange(nfil, dtype=jnp.int32))
    mixed = jnp.transpose(mixed_all, (1, 2, 0)).reshape(tokens, width)
    gated_grad = jnp.transpose(grad_all, (1, 2, 0)).reshape(tokens, width)
    scale = (tokens * (width // nfil)) ** -0.5
    filter_grad = lag_all * scale
    output = (queries.astype(jnp.float32) * mixed).astype(jnp.bfloat16)
    query_grad = (cotangent.astype(jnp.float32) * mixed).astype(jnp.bfloat16)
    key_grad = (gated_grad * values.astype(jnp.float32)).astype(jnp.bfloat16)
    value_grad = (gated_grad * keys.astype(jnp.float32)).astype(jnp.bfloat16)
    return (output, query_grad, key_grad, value_grad, filter_grad)
```

```python
import functools

import jax
import jax.numpy as jnp
from jax import lax
from jax.experimental import pallas as pl
from jax.experimental.pallas import tpu as pltpu
from jax.sharding import PartitionSpec as P

NFILT = 4
PLANES = 8
RING = 4
CTX = PLANES * RING
ROWS = 128
BLOCK = 256
NBLOCK = 16
SHARE = 32
GROUPS = 4
MESH = pl.DeviceIdType.MESH
F32 = jnp.float32
BF16 = jnp.bfloat16


def dot(a, b, ca, cb):
    return lax.dot_general(a, b, (((ca,), (cb,)), ((), ())), preferred_element_type=F32)


def kernel(nchan, scale,
           q_ref, k_ref, v_ref, taps_ref, c_ref,
           out_ref, qg_ref, kg_ref, vg_ref, fg_ref,
           sg, sb, rg, rb, om, og, bm, bg, ts, tr, toep, acc, gt_t, prod, fa, ra, sbuf, rf,
           t_ss, t_rs, g_ss, g_rs, b_ss, b_rs, m_ss, m_rs, o_ss, o_rs, a_ss, a_rs, f_ss, f_rs):
    ch = lax.axis_index("chan")
    me = lax.axis_index("ctx")
    z = lax.div(me, RING)
    y = lax.rem(me, RING)

    def peer(step):
        n = lax.div(step, RING)
        half = lax.div(n + 1, 2)
        dz = lax.rem(PLANES // 2 + PLANES + (1 - 2 * lax.rem(n, 2)) * half, PLANES)
        dy = lax.rem(step, RING)
        return lax.rem(z + dz, PLANES) * RING + lax.rem(y + dy, RING)

    def each_peer(fn):
        def body(step, carry):
            fn(peer(step))
            return carry
        lax.fori_loop(0, CTX - RING, body, 0)
        lax.fori_loop(CTX - RING + 1, CTX, body, 0)

    def each_plane_peer(fn):
        def body(step, carry):
            p = lax.rem(ch + lax.div(step, RING), nchan)
            fn(p, lax.rem(y + lax.rem(step, RING), RING))
            return carry
        lax.fori_loop(1, nchan * RING, body, 0)

    barrier = pltpu.get_barrier_semaphore()

    def greet(i):
        pl.semaphore_signal(barrier, inc=1, device_id=(ch, i), device_id_type=MESH)

    each_peer(greet)

    def greet_plane(step, carry):
        p = lax.rem(ch + lax.div(step, RING), nchan)
        pl.semaphore_signal(barrier, inc=1, device_id=(p, z * RING + lax.rem(step, RING)),
                            device_id_type=MESH)
        return carry

    lax.fori_loop(RING, nchan * RING, greet_plane, 0)

    row = lax.broadcasted_iota(jnp.int32, (128, 128), 0)
    lane = lax.broadcasted_iota(jnp.int32, (128, 128), 1)
    order = (lane == NFILT * (row % SHARE) + row // SHARE).astype(BF16)

    for f in range(NFILT):
        ts[f] = taps_ref[f:f + 1, :].astype(F32)
    for g in range(PLANES):
        at = slice(g * 128, (g + 1) * 128)
        gated = (k_ref[:, at].astype(F32) * v_ref[:, at].astype(F32)).astype(BF16)
        sg[at, :] = dot(order, gated, 1, 1).astype(BF16)
        back = (c_ref[:, at].astype(F32) * q_ref[:, at].astype(F32)).astype(BF16)
        sb[at, :] = dot(order, back, 1, 1).astype(BF16)

    pl.semaphore_wait(barrier, CTX - 1 + (nchan - 1) * RING)

    def chunk(i):
        return pl.ds(pl.multiple_of(i * SHARE, SHARE), SHARE)

    def place(i):
        return (pl.ds(pl.multiple_of(lax.div(i, 2) * SHARE, SHARE), SHARE),
                pl.ds(pl.multiple_of(lax.rem(i, 2) * 128, 128), 128))

    def copy(src, dst, ss, rs, i):
        return pltpu.make_async_remote_copy(src_ref=src, dst_ref=dst, send_sem=ss, recv_sem=rs,
                                            device_id=(ch, i), device_id_type=MESH)

    def taps_copy(i, src, slot):
        return copy(ts.at[pl.ds(lax.rem(i, RING), 1)], tr.at[pl.ds(src, 1)], t_ss.at[i], t_rs.at[slot], i)

    def in_copy(send, recv, ss, rs):
        def make(i, src, slot):
            r, l = place(src)
            return copy(send.at[chunk(i), :], recv.at[r, l], ss.at[i], rs.at[slot], i)
        return make

    def out_copy(send, recv, ss, rs):
        def make(i, src, slot):
            r, l = place(i)
            return copy(send.at[r, l], recv.at[chunk(src), :], ss.at[i], rs.at[slot], i)
        return make

    g_copy = in_copy(sg, rg, g_ss, g_rs)
    b_copy = in_copy(sb, rb, b_ss, b_rs)
    m_copy = out_copy(om, bm, m_ss, m_rs)
    o_copy = out_copy(og, bg, o_ss, o_rs)

    def send_all(make):
        each_peer(lambda i: make(i, me, me).start())

    def recv_all(make):
        each_peer(lambda i: make(i, i, i).wait_recv())

    def sent_all(make):
        each_peer(lambda i: make(i, me, me).wait_send())

    send_all(taps_copy)
    send_all(g_copy)
    send_all(b_copy)

    pad = GROUPS * SHARE
    my_rows, my_lanes = place(me)
    tr[pl.ds(me, 1)] = ts[pl.ds(y, 1)]
    rg[my_rows, my_lanes] = sg[chunk(me), :]
    rb[my_rows, my_lanes] = sb[chunk(me), :]
    rb[NBLOCK * SHARE:NBLOCK * SHARE + pad, :] = jnp.zeros((pad, BLOCK), BF16)

    recv_all(taps_copy)
    sub = lax.broadcasted_iota(jnp.int32, (BLOCK, BLOCK), 0)
    col = lax.broadcasted_iota(jnp.int32, (BLOCK, BLOCK), 1)

    def build(d, carry):
        this = jnp.concatenate([tr[2 * d], tr[2 * d + 1]], axis=1)
        low = lax.max(d - 1, 0)
        last = jnp.concatenate([tr[2 * low], tr[2 * low + 1]], axis=1)
        last = last * (d > 0).astype(F32)
        picked = jnp.where(sub + col < BLOCK, jnp.broadcast_to(this, (BLOCK, BLOCK)),
                           jnp.broadcast_to(last, (BLOCK, BLOCK)))
        toep[d] = pltpu.roll(picked, 0, 1, stride=1, stride_axis=0).astype(BF16)
        return carry

    lax.fori_loop(0, NBLOCK, build, 0)

    full = NBLOCK * SHARE
    recv_all(g_copy)
    for d in range(NBLOCK):
        part = dot(rg[0:full - SHARE * d, :], toep[d], 1, 0)
        if d == 0:
            acc[...] = part
        else:
            acc[SHARE * d:full, :] += part
    om[...] = acc[...].astype(BF16)
    send_all(m_copy)
    bm[chunk(me), :] = om[my_rows, my_lanes]

    recv_all(b_copy)
    for d in range(NBLOCK):
        part = dot(rb[SHARE * d:full, :], toep[d], 1, 1)
        if d == 0:
            acc[...] = part
        else:
            acc[0:full - SHARE * d, :] += part
    og[...] = acc[...].astype(BF16)
    send_all(o_copy)
    bg[chunk(me), :] = og[my_rows, my_lanes]

    flip = (sub + col == BLOCK - 1).astype(BF16)
    gt_t[...] = dot(flip, rg[...], 1, 1).astype(BF16)
    for group in range(NBLOCK // GROUPS):
        depth = full - group * GROUPS * SHARE
        for s in range(GROUPS):
            d = group * GROUPS + s
            prod[d] = dot(gt_t[:, 0:depth], rb[SHARE * d:SHARE * d + depth, :], 1, 0)
    prod[NBLOCK] = jnp.zeros((BLOCK, BLOCK), F32)

    def lag_sums(plane, carry):
        for e in range(2):
            d = 2 * plane + e
            both = jnp.where(col + sub >= BLOCK - 1, prod[d], prod[d + 1])
            sums = jnp.sum(pltpu.roll(both, 1, 1, stride=1, stride_axis=0), axis=0, keepdims=True)
            fa[RING * plane + 2 * e] = sums[:, 0:128]
            fa[RING * plane + 2 * e + 1] = sums[:, 128:256]
        return carry

    lax.fori_loop(0, PLANES, lag_sums, 0)

    def a_copy(p, src, slot):
        return copy(fa.at[pl.ds(RING * p, RING)], ra.at[src], a_ss.at[p], a_rs.at[slot], RING * p + y)

    def planes(fn):
        def body(step, carry):
            fn(lax.rem(z + step, PLANES))
            return carry
        lax.fori_loop(1, PLANES, body, 0)

    planes(lambda p: a_copy(p, z, z).start())
    ra[z] = fa[pl.ds(RING * z, RING)]

    recv_all(m_copy)
    for g in range(PLANES):
        at = slice(g * 128, (g + 1) * 128)
        mixed = dot(bm[at, :], order, 0, 0)
        out_ref[:, at] = (q_ref[:, at].astype(F32) * mixed).astype(BF16)
        qg_ref[:, at] = (c_ref[:, at].astype(F32) * mixed).astype(BF16)

    planes(lambda p: a_copy(p, p, p).wait_recv())
    total = ra[0]
    for p in range(1, PLANES):
        total = total + ra[p]
    sbuf[...] = total

    def f_copy(p, r, srcp, srcf):
        slot = srcp * RING + srcf
        return pltpu.make_async_remote_copy(
            src_ref=sbuf.at[pl.ds(r, 1)], dst_ref=rf.at[pl.ds(slot, 1)],
            send_sem=f_ss.at[p * RING + r], recv_sem=f_rs.at[slot],
            device_id=(p, z * RING + r), device_id_type=MESH)

    each_plane_peer(lambda p, r: f_copy(p, r, ch, y).start())
    rf[pl.ds(ch * RING + y, 1)] = sbuf[pl.ds(y, 1)]

    recv_all(o_copy)
    for g in range(PLANES):
        at = slice(g * 128, (g + 1) * 128)
        grad = dot(bg[at, :], order, 0, 0)
        kg_ref[:, at] = (grad * v_ref[:, at].astype(F32)).astype(BF16)
        vg_ref[:, at] = (grad * k_ref[:, at].astype(F32)).astype(BF16)

    each_plane_peer(lambda p, r: f_copy(p, r, p, r).wait_recv())
    for f in range(NFILT):
        total = rf[f]
        for p in range(1, nchan):
            total = total + rf[p * RING + f]
        fg_ref[f:f + 1, :] = total * scale

    sent_all(taps_copy)
    sent_all(g_copy)
    sent_all(b_copy)
    sent_all(m_copy)
    sent_all(o_copy)
    planes(lambda p: a_copy(p, z, z).wait_send())
    each_plane_peer(lambda p, r: f_copy(p, r, ch, y).wait_send())


def shards(nchan, queries, keys, values, filters, cotangent):
    rows, width = queries.shape
    tokens = rows * CTX
    scale = (tokens * (nchan * width // NFILT)) ** (-0.5)
    vmem = pl.BlockSpec(memory_space=pltpu.VMEM)
    dma = pltpu.SemaphoreType.DMA
    full = NBLOCK * SHARE
    act = jax.ShapeDtypeStruct((rows, width), BF16)
    return pl.pallas_call(
        functools.partial(kernel, nchan, scale),
        out_shape=(act, act, act, act, jax.ShapeDtypeStruct((NFILT, rows), F32)),
        in_specs=[vmem] * 5,
        out_specs=[vmem] * 5,
        scratch_shapes=[
            pltpu.VMEM((width, rows), BF16),
            pltpu.VMEM((width, rows), BF16),
            pltpu.VMEM((full, BLOCK), BF16),
            pltpu.VMEM((full + GROUPS * SHARE, BLOCK), BF16),
            pltpu.VMEM((full, BLOCK), BF16),
            pltpu.VMEM((full, BLOCK), BF16),
            pltpu.VMEM((width, rows), BF16),
            pltpu.VMEM((width, rows), BF16),
            pltpu.VMEM((NFILT, 1, rows), F32),
            pltpu.VMEM((CTX, 1, rows), F32),
            pltpu.VMEM((NBLOCK, BLOCK, BLOCK), BF16),
            pltpu.VMEM((full, BLOCK), F32),
            pltpu.VMEM((BLOCK, full), BF16),
            pltpu.VMEM((NBLOCK + 1, BLOCK, BLOCK), F32),
            pltpu.VMEM((CTX, 1, rows), F32),
            pltpu.VMEM((PLANES, RING, 1, rows), F32),
            pltpu.VMEM((RING, 1, rows), F32),
            pltpu.VMEM((nchan * RING, 1, rows), F32),
        ] + [dma((CTX,))] * 10 + [dma((PLANES,))] * 2 + [dma((nchan * RING,))] * 2,
        compiler_params=pltpu.CompilerParams(
            collective_id=0, has_side_effects=True, vmem_limit_bytes=40 * 1024 * 1024
        ),
    )(queries, keys, values, filters, cotangent)


def solution(mesh):
    act = P("ctx", "chan")
    taps = P(None, "ctx")
    return jax.shard_map(
        functools.partial(shards, mesh.shape["chan"]),
        mesh=mesh,
        in_specs=(act, act, act, taps, act),
        out_specs=(act, act, act, act, taps),
        check_vma=False,
    )
```

```python
import functools

import jax
import jax.numpy as jnp
from jax import lax
from jax.experimental import pallas as pl
from jax.experimental.pallas import tpu as pltpu
from jax.sharding import PartitionSpec as P

NFILT = 4
PLANES = 8
RING = 4
CTX = PLANES * RING
ROWS = 128
BLOCK = 256
NBLOCK = 16
SHARE = 32
GROUPS = 4
MESH = pl.DeviceIdType.MESH
F32 = jnp.float32
BF16 = jnp.bfloat16


def dot(a, b, ca, cb):
    return lax.dot_general(a, b, (((ca,), (cb,)), ((), ())), preferred_element_type=F32)


def kernel(nchan, scale,
           q_hbm, k_hbm, v_hbm, taps_hbm, c_hbm,
           out_ref, qg_ref, kg_ref, vg_ref, fg_ref,
           q_ref, k_ref, v_ref, taps_ref, c_ref, load_sem,
           sg, sb, rg, rb, om, og, bm, bg, ts, tr, toep, acc, gt_t, prod, fa, ra, sbuf, rf,
           t_ss, t_rs, g_ss, g_rs, b_ss, b_rs, m_ss, m_rs, o_ss, o_rs, a_ss, a_rs, f_ss, f_rs):
    ch = lax.axis_index("chan")
    me = lax.axis_index("ctx")
    z = lax.div(me, RING)
    y = lax.rem(me, RING)

    def peer(step):
        n = lax.div(step, RING)
        half = lax.div(n + 1, 2)
        dz = lax.rem(PLANES // 2 + PLANES + (1 - 2 * lax.rem(n, 2)) * half, PLANES)
        dy = lax.rem(step, RING)
        return lax.rem(z + dz, PLANES) * RING + lax.rem(y + dy, RING)

    def each_peer(fn):
        def body(step, carry):
            fn(peer(step))
            return carry
        lax.fori_loop(0, CTX - RING, body, 0)
        lax.fori_loop(CTX - RING + 1, CTX, body, 0)

    def each_plane_peer(fn):
        def body(step, carry):
            p = lax.rem(ch + lax.div(step, RING), nchan)
            fn(p, lax.rem(y + lax.rem(step, RING), RING))
            return carry
        lax.fori_loop(1, nchan * RING, body, 0)

    barrier = pltpu.get_barrier_semaphore()

    def greet(i):
        pl.semaphore_signal(barrier, inc=1, device_id=(ch, i), device_id_type=MESH)

    each_peer(greet)

    def greet_plane(step, carry):
        p = lax.rem(ch + lax.div(step, RING), nchan)
        pl.semaphore_signal(barrier, inc=1, device_id=(p, z * RING + lax.rem(step, RING)),
                            device_id_type=MESH)
        return carry

    lax.fori_loop(RING, nchan * RING, greet_plane, 0)

    loads = [pltpu.make_async_copy(src, dst, load_sem.at[n]) for n, (src, dst) in enumerate((
        (k_hbm, k_ref), (v_hbm, v_ref), (c_hbm, c_ref), (q_hbm, q_ref), (taps_hbm, taps_ref)))]
    for load in loads:
        load.start()

    row = lax.broadcasted_iota(jnp.int32, (128, 128), 0)
    lane = lax.broadcasted_iota(jnp.int32, (128, 128), 1)
    order = (lane == NFILT * (row % SHARE) + row // SHARE).astype(BF16)

    for load in loads:
        load.wait()
    for f in range(NFILT):
        ts[f] = taps_ref[f:f + 1, :].astype(F32)
    for g in range(PLANES):
        at = slice(g * 128, (g + 1) * 128)
        gated = (k_ref[:, at].astype(F32) * v_ref[:, at].astype(F32)).astype(BF16)
        sg[at, :] = dot(order, gated, 1, 1).astype(BF16)
        back = (c_ref[:, at].astype(F32) * q_ref[:, at].astype(F32)).astype(BF16)
        sb[at, :] = dot(order, back, 1, 1).astype(BF16)

    pl.semaphore_wait(barrier, CTX - 1 + (nchan - 1) * RING)

    def chunk(i):
        return pl.ds(pl.multiple_of(i * SHARE, SHARE), SHARE)

    def place(i):
        return (pl.ds(pl.multiple_of(lax.div(i, 2) * SHARE, SHARE), SHARE),
                pl.ds(pl.multiple_of(lax.rem(i, 2) * 128, 128), 128))

    def copy(src, dst, ss, rs, i):
        return pltpu.make_async_remote_copy(src_ref=src, dst_ref=dst, send_sem=ss, recv_sem=rs,
                                            device_id=(ch, i), device_id_type=MESH)

    def taps_copy(i, src, slot):
        return copy(ts.at[pl.ds(lax.rem(i, RING), 1)], tr.at[pl.ds(src, 1)], t_ss.at[i], t_rs.at[slot], i)

    def in_copy(send, recv, ss, rs):
        def make(i, src, slot):
            r, l = place(src)
            return copy(send.at[chunk(i), :], recv.at[r, l], ss.at[i], rs.at[slot], i)
        return make

    def out_copy(send, recv, ss, rs):
        def make(i, src, slot):
            r, l = place(i)
            return copy(send.at[r, l], recv.at[chunk(src), :], ss.at[i], rs.at[slot], i)
        return make

    g_copy = in_copy(sg, rg, g_ss, g_rs)
    b_copy = in_copy(sb, rb, b_ss, b_rs)
    m_copy = out_copy(om, bm, m_ss, m_rs)
    o_copy = out_copy(og, bg, o_ss, o_rs)

    def send_all(make):
        each_peer(lambda i: make(i, me, me).start())

    def recv_all(make):
        each_peer(lambda i: make(i, i, i).wait_recv())

    def sent_all(make):
        each_peer(lambda i: make(i, me, me).wait_send())

    send_all(taps_copy)
    send_all(g_copy)
    send_all(b_copy)

    pad = GROUPS * SHARE
    my_rows, my_lanes = place(me)
    tr[pl.ds(me, 1)] = ts[pl.ds(y, 1)]
    rg[my_rows, my_lanes] = sg[chunk(me), :]
    rb[my_rows, my_lanes] = sb[chunk(me), :]
    rb[NBLOCK * SHARE:NBLOCK * SHARE + pad, :] = jnp.zeros((pad, BLOCK), BF16)

    recv_all(taps_copy)
    sub = lax.broadcasted_iota(jnp.int32, (BLOCK, BLOCK), 0)
    col = lax.broadcasted_iota(jnp.int32, (BLOCK, BLOCK), 1)

    def build(d, carry):
        this = jnp.concatenate([tr[2 * d], tr[2 * d + 1]], axis=1)
        low = lax.max(d - 1, 0)
        last = jnp.concatenate([tr[2 * low], tr[2 * low + 1]], axis=1)
        last = last * (d > 0).astype(F32)
        picked = jnp.where(sub + col < BLOCK, jnp.broadcast_to(this, (BLOCK, BLOCK)),
                           jnp.broadcast_to(last, (BLOCK, BLOCK)))
        toep[d] = pltpu.roll(picked, 0, 1, stride=1, stride_axis=0).astype(BF16)
        return carry

    lax.fori_loop(0, NBLOCK, build, 0)

    full = NBLOCK * SHARE
    recv_all(g_copy)
    for d in range(NBLOCK):
        part = dot(rg[0:full - SHARE * d, :], toep[d], 1, 0)
        if d == 0:
            acc[...] = part
        else:
            acc[SHARE * d:full, :] += part
    om[...] = acc[...].astype(BF16)
    send_all(m_copy)
    bm[chunk(me), :] = om[my_rows, my_lanes]

    recv_all(b_copy)
    flip = (sub + col == BLOCK - 1).astype(BF16)
    gt_t[...] = dot(flip, rg[...], 1, 1).astype(BF16)
    for group in range(NBLOCK // GROUPS):
        depth = full - group * GROUPS * SHARE
        for s in range(GROUPS):
            d = group * GROUPS + s
            prod[d] = dot(gt_t[:, 0:depth], rb[SHARE * d:SHARE * d + depth, :], 1, 0)
    prod[NBLOCK] = jnp.zeros((BLOCK, BLOCK), F32)

    def lag_sums(plane, carry):
        for e in range(2):
            d = 2 * plane + e
            both = jnp.where(col + sub >= BLOCK - 1, prod[d], prod[d + 1])
            sums = jnp.sum(pltpu.roll(both, 1, 1, stride=1, stride_axis=0), axis=0, keepdims=True)
            fa[RING * plane + 2 * e] = sums[:, 0:128]
            fa[RING * plane + 2 * e + 1] = sums[:, 128:256]
        return carry

    lax.fori_loop(0, PLANES, lag_sums, 0)

    def a_copy(p, src, slot):
        return copy(fa.at[pl.ds(RING * p, RING)], ra.at[src], a_ss.at[p], a_rs.at[slot], RING * p + y)

    def planes(fn):
        def body(step, carry):
            fn(lax.rem(z + step, PLANES))
            return carry
        lax.fori_loop(1, PLANES, body, 0)

    planes(lambda p: a_copy(p, z, z).start())
    ra[z] = fa[pl.ds(RING * z, RING)]

    for d in range(NBLOCK):
        part = dot(rb[SHARE * d:full, :], toep[d], 1, 1)
        if d == 0:
            acc[...] = part
        else:
            acc[0:full - SHARE * d, :] += part
    og[...] = acc[...].astype(BF16)
    send_all(o_copy)
    bg[chunk(me), :] = og[my_rows, my_lanes]

    def tiles(make, fn):
        def pieces(step, carry):
            i = peer(step)
            make(i, i, i).wait_recv()
            return carry

        def body(n, carry):
            lax.fori_loop(RING * n, RING * n + RING, pieces, 0)
            g = lax.div(peer(RING * n), RING)
            fn(pl.ds(pl.multiple_of(g * 128, 128), 128))
            return carry

        lax.fori_loop(0, PLANES - 1, body, 0)
        lax.fori_loop(CTX - RING + 1, CTX, pieces, 0)
        fn(pl.ds(pl.multiple_of(z * 128, 128), 128))

    def finish_mixed(at):
        mixed = dot(bm[at, :], order, 0, 0)
        out_ref[:, at] = (q_ref[:, at].astype(F32) * mixed).astype(BF16)
        qg_ref[:, at] = (c_ref[:, at].astype(F32) * mixed).astype(BF16)

    def finish_grad(at):
        grad = dot(bg[at, :], order, 0, 0)
        kg_ref[:, at] = (grad * v_ref[:, at].astype(F32)).astype(BF16)
        vg_ref[:, at] = (grad * k_ref[:, at].astype(F32)).astype(BF16)

    tiles(m_copy, finish_mixed)

    planes(lambda p: a_copy(p, p, p).wait_recv())
    total = ra[0]
    for p in range(1, PLANES):
        total = total + ra[p]
    sbuf[...] = total

    def f_copy(p, r, srcp, srcf):
        slot = srcp * RING + srcf
        return pltpu.make_async_remote_copy(
            src_ref=sbuf.at[pl.ds(r, 1)], dst_ref=rf.at[pl.ds(slot, 1)],
            send_sem=f_ss.at[p * RING + r], recv_sem=f_rs.at[slot],
            device_id=(p, z * RING + r), device_id_type=MESH)

    each_plane_peer(lambda p, r: f_copy(p, r, ch, y).start())
    rf[pl.ds(ch * RING + y, 1)] = sbuf[pl.ds(y, 1)]

    tiles(o_copy, finish_grad)

    each_plane_peer(lambda p, r: f_copy(p, r, p, r).wait_recv())
    for f in range(NFILT):
        total = rf[f]
        for p in range(1, nchan):
            total = total + rf[p * RING + f]
        fg_ref[f:f + 1, :] = total * scale

    sent_all(taps_copy)
    sent_all(g_copy)
    sent_all(b_copy)
    sent_all(m_copy)
    sent_all(o_copy)
    planes(lambda p: a_copy(p, z, z).wait_send())
    each_plane_peer(lambda p, r: f_copy(p, r, ch, y).wait_send())


def store(*refs):
    sems = refs[10]
    copies = [pltpu.make_async_copy(refs[n], refs[5 + n], sems.at[n]) for n in range(5)]
    for item in copies:
        item.start()
    for item in copies:
        item.wait()


def shards(nchan, queries, keys, values, filters, cotangent):
    rows, width = queries.shape
    tokens = rows * CTX
    scale = (tokens * (nchan * width // NFILT)) ** (-0.5)
    vmem = pl.BlockSpec(memory_space=pltpu.VMEM)
    dma = pltpu.SemaphoreType.DMA
    full = NBLOCK * SHARE
    act = jax.ShapeDtypeStruct((rows, width), BF16)
    queries, keys, values, filters, cotangent = [pltpu.with_memory_space_constraint(x, pltpu.HBM) for x in (queries, keys, values, filters, cotangent)]
    held = pl.pallas_call(
        functools.partial(kernel, nchan, scale),
        out_shape=(act, act, act, act, jax.ShapeDtypeStruct((NFILT, rows), F32)),
        in_specs=[pl.BlockSpec(memory_space=pltpu.HBM)] * 5,
        out_specs=[vmem] * 5,
        scratch_shapes=[
            pltpu.VMEM((rows, width), BF16),
            pltpu.VMEM((rows, width), BF16),
            pltpu.VMEM((rows, width), BF16),
            pltpu.VMEM((NFILT, rows), BF16),
            pltpu.VMEM((rows, width), BF16),
            dma((5,)),
            pltpu.VMEM((width, rows), BF16),
            pltpu.VMEM((width, rows), BF16),
            pltpu.VMEM((full, BLOCK), BF16),
            pltpu.VMEM((full + GROUPS * SHARE, BLOCK), BF16),
            pltpu.VMEM((full, BLOCK), BF16),
            pltpu.VMEM((full, BLOCK), BF16),
            pltpu.VMEM((width, rows), BF16),
            pltpu.VMEM((width, rows), BF16),
            pltpu.VMEM((NFILT, 1, rows), F32),
            pltpu.VMEM((CTX, 1, rows), F32),
            pltpu.VMEM((NBLOCK, BLOCK, BLOCK), BF16),
            pltpu.VMEM((full, BLOCK), F32),
            pltpu.VMEM((BLOCK, full), BF16),
            pltpu.VMEM((NBLOCK + 1, BLOCK, BLOCK), F32),
            pltpu.VMEM((CTX, 1, rows), F32),
            pltpu.VMEM((PLANES, RING, 1, rows), F32),
            pltpu.VMEM((RING, 1, rows), F32),
            pltpu.VMEM((nchan * RING, 1, rows), F32),
        ] + [dma((CTX,))] * 10 + [dma((PLANES,))] * 2 + [dma((nchan * RING,))] * 2,
        compiler_params=pltpu.CompilerParams(
            collective_id=0, has_side_effects=True, vmem_limit_bytes=40000000
        ),
    )(queries, keys, values, filters, cotangent)
    return pl.pallas_call(
        store,
        out_shape=(act, act, act, act, jax.ShapeDtypeStruct((NFILT, rows), F32)),
        in_specs=[vmem] * 5,
        out_specs=[pl.BlockSpec(memory_space=pltpu.HBM)] * 5,
        scratch_shapes=[dma((5,))],
        compiler_params=pltpu.CompilerParams(vmem_limit_bytes=4 * 1024 * 1024),
    )(*held)


def solution(mesh):
    act = P("ctx", "chan")
    taps = P(None, "ctx")
    return jax.shard_map(
        functools.partial(shards, mesh.shape["chan"]),
        mesh=mesh,
        in_specs=(act, act, act, taps, act),
        out_specs=(act, act, act, act, taps),
        check_vma=False,
    )
```

```python
import functools

import jax
import jax.numpy as jnp
from jax import lax
from jax.experimental import pallas as pl
from jax.experimental.pallas import tpu as pltpu
from jax.sharding import PartitionSpec as P

NFILT = 4
PLANES = 8
RING = 4
CTX = PLANES * RING
ROWS = 128
BLOCK = 256
NBLOCK = 16
SHARE = 32
GROUPS = 4
MESH = pl.DeviceIdType.MESH
F32 = jnp.float32
BF16 = jnp.bfloat16


def dot(a, b, ca, cb):
    return lax.dot_general(a, b, (((ca,), (cb,)), ((), ())), preferred_element_type=F32)


def kernel(nchan, scale,
           q_hbm, k_hbm, v_hbm, taps_hbm, c_hbm,
           out_ref, qg_ref, kg_ref, vg_ref, fg_ref,
           q_ref, k_ref, v_ref, taps_ref, c_ref, load_sem,
           sg, sb, rg, rb, om, og, bm, bg, ts, tr, toep, acc, gt_t, prod, fa, ra, sbuf, rf,
           send_sem, t_rs, g_rs, b_rs, m_rs, o_rs, a_rs, f_rs):
    ch = lax.axis_index("chan")
    me = lax.axis_index("ctx")
    z = lax.div(me, RING)
    y = lax.rem(me, RING)
    zs = [z] + [lax.rem(z + dz, PLANES) for dz in range(1, PLANES)]
    ys = [y] + [lax.rem(y + dy, RING) for dy in range(1, RING)]
    ps = [ch] + [lax.rem(ch + p, nchan) for p in range(1, nchan)]
    planes = (4, 3, 5, 2, 6, 1, 7, 0)
    peers = [(dz, dy) for dz in planes for dy in range(RING) if dz or dy]
    near = [(p, dy) for p in range(nchan) for dy in range(RING) if p or dy]

    barrier = pltpu.get_barrier_semaphore()

    def greet(p, dz, dy):
        pl.semaphore_signal(barrier, inc=1, device_id=(ps[p], zs[dz] * RING + ys[dy]), device_id_type=MESH)

    for dz, dy in peers:
        greet(0, dz, dy)
    for p in range(1, nchan):
        for dy in range(RING):
            greet(p, 0, dy)

    loads = [pltpu.make_async_copy(src, dst, load_sem.at[n]) for n, (src, dst) in enumerate((
        (k_hbm, k_ref), (v_hbm, v_ref), (c_hbm, c_ref), (q_hbm, q_ref), (taps_hbm, taps_ref)))]
    for load in loads:
        load.start()

    row = lax.broadcasted_iota(jnp.int32, (128, 128), 0)
    lane = lax.broadcasted_iota(jnp.int32, (128, 128), 1)
    order = (lane == NFILT * (row % SHARE) + row // SHARE).astype(BF16)

    for load in loads:
        load.wait()
    for f in range(NFILT):
        ts[f] = taps_ref[f:f + 1, :].astype(F32)
    for g in range(PLANES):
        at = slice(g * 128, (g + 1) * 128)
        gated = (k_ref[:, at].astype(F32) * v_ref[:, at].astype(F32)).astype(BF16)
        sg[at, :] = dot(order, gated, 1, 1).astype(BF16)
        back = (c_ref[:, at].astype(F32) * q_ref[:, at].astype(F32)).astype(BF16)
        sb[at, :] = dot(order, back, 1, 1).astype(BF16)

    pl.semaphore_wait(barrier, CTX - 1 + (nchan - 1) * RING)

    def chunk(i):
        return pl.ds(pl.multiple_of(i * SHARE, SHARE), SHARE)

    def place(i):
        return (pl.ds(pl.multiple_of(lax.div(i, 2) * SHARE, SHARE), SHARE),
                pl.ds(pl.multiple_of(lax.rem(i, 2) * 128, 128), 128))

    my_rows, my_lanes = place(me)
    places = {(dz, dy): place(zs[dz] * RING + ys[dy]) for dz, dy in peers}

    def copy(src, dst, n, recv, p, dz, dy):
        return pltpu.make_async_remote_copy(
            src_ref=src, dst_ref=dst, send_sem=send_sem.at[n], recv_sem=recv,
            device_id=(ps[p], zs[dz] * RING + ys[dy]), device_id_type=MESH)

    def arrived(like, recv):
        copy(like, like, 0, recv, 0, 1, 0).wait_recv()

    def sent(like, n):
        copy(like, like, n, t_rs.at[0], 0, 1, 0).wait_send()

    def send_in(send, recv, n, rs):
        for dz, dy in peers:
            copy(send.at[chunk(zs[dz] * RING + ys[dy]), :], recv.at[my_rows, my_lanes], n, rs.at[0], 0, dz, dy).start()

    def send_out(send, recv, n, rs):
        for dz, dy in peers:
            r, l = places[dz, dy]
            copy(send.at[r, l], recv.at[chunk(me), :], n, rs.at[(PLANES - dz) % PLANES], 0, dz, dy).start()

    others = pl.ds(0, (CTX - 1) * SHARE)
    for dz, dy in peers:
        copy(ts.at[pl.ds(ys[dy], 1)], tr.at[pl.ds(me, 1)], 0, t_rs.at[0], 0, dz, dy).start()
    send_in(sg, rg, 1, g_rs)
    send_in(sb, rb, 2, b_rs)

    pad = GROUPS * SHARE
    tr[pl.ds(me, 1)] = ts[pl.ds(y, 1)]
    rg[my_rows, my_lanes] = sg[chunk(me), :]
    rb[my_rows, my_lanes] = sb[chunk(me), :]
    rb[NBLOCK * SHARE:NBLOCK * SHARE + pad, :] = jnp.zeros((pad, BLOCK), BF16)

    arrived(tr.at[pl.ds(0, CTX - 1)], t_rs.at[0])
    sub = lax.broadcasted_iota(jnp.int32, (BLOCK, BLOCK), 0)
    col = lax.broadcasted_iota(jnp.int32, (BLOCK, BLOCK), 1)

    def build(d, carry):
        this = jnp.concatenate([tr[2 * d], tr[2 * d + 1]], axis=1)
        low = lax.max(d - 1, 0)
        last = jnp.concatenate([tr[2 * low], tr[2 * low + 1]], axis=1)
        last = last * (d > 0).astype(F32)
        picked = jnp.where(sub + col < BLOCK, jnp.broadcast_to(this, (BLOCK, BLOCK)),
                           jnp.broadcast_to(last, (BLOCK, BLOCK)))
        toep[d] = pltpu.roll(picked, 0, 1, stride=1, stride_axis=0).astype(BF16)
        return carry

    lax.fori_loop(0, NBLOCK, build, 0)

    full = NBLOCK * SHARE
    arrived(sg.at[others], g_rs.at[0])
    for d in range(NBLOCK):
        part = dot(rg[0:full - SHARE * d, :], toep[d], 1, 0)
        if d == 0:
            acc[...] = part
        else:
            acc[SHARE * d:full, :] += part
    om[...] = acc[...].astype(BF16)
    send_out(om, bm, 3, m_rs)
    bm[chunk(me), :] = om[my_rows, my_lanes]

    flip = (sub + col == BLOCK - 1).astype(BF16)
    gt_t[...] = dot(flip, rg[...], 1, 1).astype(BF16)
    arrived(sb.at[others], b_rs.at[0])
    for group in range(NBLOCK // GROUPS):
        depth = full - group * GROUPS * SHARE
        for s in range(GROUPS):
            d = group * GROUPS + s
            prod[d] = dot(gt_t[:, 0:depth], rb[SHARE * d:SHARE * d + depth, :], 1, 0)
    prod[NBLOCK] = jnp.zeros((BLOCK, BLOCK), F32)

    def lag_sums(plane, carry):
        for e in range(2):
            d = 2 * plane + e
            both = jnp.where(col + sub >= BLOCK - 1, prod[d], prod[d + 1])
            sums = jnp.sum(pltpu.roll(both, 1, 1, stride=1, stride_axis=0), axis=0, keepdims=True)
            fa[RING * plane + 2 * e] = sums[:, 0:128]
            fa[RING * plane + 2 * e + 1] = sums[:, 128:256]
        return carry

    lax.fori_loop(0, PLANES, lag_sums, 0)

    for dz in planes[:-1]:
        copy(fa.at[pl.ds(RING * zs[dz], RING)], ra.at[z], 5, a_rs.at[0], 0, dz, 0).start()
    ra[z] = fa[pl.ds(RING * z, RING)]

    for d in range(NBLOCK):
        part = dot(rb[SHARE * d:full, :], toep[d], 1, 1)
        if d == 0:
            acc[...] = part
        else:
            acc[0:full - SHARE * d, :] += part
    og[...] = acc[...].astype(BF16)
    send_out(og, bg, 4, o_rs)
    bg[chunk(me), :] = og[my_rows, my_lanes]

    def tiles(recv, rs, fn):
        for dz in planes:
            arrived(recv.at[pl.ds(0, (RING - (dz == 0)) * SHARE), :], rs.at[dz])
            rows = pl.ds(pl.multiple_of(zs[dz] * 128, 128), 128)
            fn(dot(recv[rows, :], order, 0, 0), rows)

    def finish_mixed(mixed, at):
        out_ref[:, at] = (q_ref[:, at].astype(F32) * mixed).astype(BF16)
        qg_ref[:, at] = (c_ref[:, at].astype(F32) * mixed).astype(BF16)

    def finish_grad(grad, at):
        kg_ref[:, at] = (grad * v_ref[:, at].astype(F32)).astype(BF16)
        vg_ref[:, at] = (grad * k_ref[:, at].astype(F32)).astype(BF16)

    arrived(fa.at[pl.ds(0, (PLANES - 1) * RING)], a_rs.at[0])
    total = ra[0]
    for p in range(1, PLANES):
        total = total + ra[p]
    sbuf[...] = total
    for p, dy in near:
        copy(sbuf.at[pl.ds(ys[dy], 1)], rf.at[pl.ds(ch * RING + y, 1)], 6, f_rs.at[0], p, 0, dy).start()
    rf[pl.ds(ch * RING + y, 1)] = sbuf[pl.ds(y, 1)]

    tiles(bm, m_rs, finish_mixed)
    tiles(bg, o_rs, finish_grad)

    arrived(rf.at[pl.ds(0, nchan * RING - 1)], f_rs.at[0])
    for f in range(NFILT):
        total = rf[f]
        for p in range(1, nchan):
            total = total + rf[p * RING + f]
        fg_ref[f:f + 1, :] = total * scale

    sent(tr.at[pl.ds(0, CTX - 1)], 0)
    for n in range(1, 5):
        sent(sg.at[others], n)
    sent(fa.at[pl.ds(0, (PLANES - 1) * RING)], 5)
    sent(rf.at[pl.ds(0, nchan * RING - 1)], 6)


def store(*refs):
    sems = refs[10]
    copies = [pltpu.make_async_copy(refs[n], refs[5 + n], sems.at[n]) for n in range(5)]
    for item in copies:
        item.start()
    for item in copies:
        item.wait()


def shards(nchan, queries, keys, values, filters, cotangent):
    rows, width = queries.shape
    tokens = rows * CTX
    scale = (tokens * (nchan * width // NFILT)) ** (-0.5)
    vmem = pl.BlockSpec(memory_space=pltpu.VMEM)
    dma = pltpu.SemaphoreType.DMA
    full = NBLOCK * SHARE
    act = jax.ShapeDtypeStruct((rows, width), BF16)
    queries, keys, values, filters, cotangent = [pltpu.with_memory_space_constraint(x, pltpu.HBM) for x in (queries, keys, values, filters, cotangent)]
    held = pl.pallas_call(
        functools.partial(kernel, nchan, scale),
        out_shape=(act, act, act, act, jax.ShapeDtypeStruct((NFILT, rows), F32)),
        in_specs=[pl.BlockSpec(memory_space=pltpu.HBM)] * 5,
        out_specs=[vmem] * 5,
        scratch_shapes=[
            pltpu.VMEM((rows, width), BF16),
            pltpu.VMEM((rows, width), BF16),
            pltpu.VMEM((rows, width), BF16),
            pltpu.VMEM((NFILT, rows), BF16),
            pltpu.VMEM((rows, width), BF16),
            dma((5,)),
            pltpu.VMEM((width, rows), BF16),
            pltpu.VMEM((width, rows), BF16),
            pltpu.VMEM((full, BLOCK), BF16),
            pltpu.VMEM((full + GROUPS * SHARE, BLOCK), BF16),
            pltpu.VMEM((full, BLOCK), BF16),
            pltpu.VMEM((full, BLOCK), BF16),
            pltpu.VMEM((width, rows), BF16),
            pltpu.VMEM((width, rows), BF16),
            pltpu.VMEM((NFILT, 1, rows), F32),
            pltpu.VMEM((CTX, 1, rows), F32),
            pltpu.VMEM((NBLOCK, BLOCK, BLOCK), BF16),
            pltpu.VMEM((full, BLOCK), F32),
            pltpu.VMEM((BLOCK, full), BF16),
            pltpu.VMEM((NBLOCK + 1, BLOCK, BLOCK), F32),
            pltpu.VMEM((CTX, 1, rows), F32),
            pltpu.VMEM((PLANES, RING, 1, rows), F32),
            pltpu.VMEM((RING, 1, rows), F32),
            pltpu.VMEM((nchan * RING, 1, rows), F32),
        ] + [dma((7,))] + [dma((1,))] * 3 + [dma((PLANES,))] * 2 + [dma((1,))] * 2,
        compiler_params=pltpu.CompilerParams(
            collective_id=0, has_side_effects=True, vmem_limit_bytes=40000000
        ),
    )(queries, keys, values, filters, cotangent)
    return pl.pallas_call(
        store,
        out_shape=(act, act, act, act, jax.ShapeDtypeStruct((NFILT, rows), F32)),
        in_specs=[vmem] * 5,
        out_specs=[pl.BlockSpec(memory_space=pltpu.HBM)] * 5,
        scratch_shapes=[dma((5,))],
        compiler_params=pltpu.CompilerParams(vmem_limit_bytes=4 * 1024 * 1024),
    )(*held)


def solution(mesh):
    act = P("ctx", "chan")
    taps = P(None, "ctx")
    return jax.shard_map(
        functools.partial(shards, mesh.shape["chan"]),
        mesh=mesh,
        in_specs=(act, act, act, taps, act),
        out_specs=(act, act, act, act, taps),
        check_vma=False,
    )
```

```python
import functools

import jax
import jax.numpy as jnp
from jax import lax
from jax.experimental import pallas as pl
from jax.experimental.pallas import tpu as pltpu
from jax.sharding import PartitionSpec as P

NFILT = 4
PLANES = 8
RING = 4
CTX = PLANES * RING
ROWS = 128
BLOCK = 256
NBLOCK = 16
SHARE = 32
GROUPS = 4
MESH = pl.DeviceIdType.MESH
F32 = jnp.float32
BF16 = jnp.bfloat16


def dot(a, b, ca, cb):
    return lax.dot_general(a, b, (((ca,), (cb,)), ((), ())), preferred_element_type=F32)


def kernel(nchan, scale,
           q_hbm, k_hbm, v_hbm, taps_hbm, c_hbm,
           out_ref, qg_ref, kg_ref, vg_ref, fg_ref,
           q_ref, k_ref, v_ref, taps_ref, c_ref, load_sem,
           sg, sb, rg, rb, om, og, bm, bg, ts, tr, toep, acc, gt_t, prod, fa, ra, sbuf, rf,
           send_sem, t_rs, g_rs, b_rs, m_rs, o_rs, a_rs, f_rs):
    ch = lax.axis_index("chan")
    me = lax.axis_index("ctx")
    z = lax.div(me, RING)
    y = lax.rem(me, RING)
    zs = [z] + [lax.rem(z + dz, PLANES) for dz in range(1, PLANES)]
    ys = [y] + [lax.rem(y + dy, RING) for dy in range(1, RING)]
    ps = [ch] + [lax.rem(ch + p, nchan) for p in range(1, nchan)]
    planes = (4, 3, 5, 2, 6, 1, 7, 0)
    peers = [(dz, dy) for dz in planes for dy in range(RING) if dz or dy]
    near = [(p, dy) for p in range(nchan) for dy in range(RING) if p or dy]

    barrier = pltpu.get_barrier_semaphore()

    def greet(p, dz, dy):
        pl.semaphore_signal(barrier, inc=1, device_id=(ps[p], zs[dz] * RING + ys[dy]), device_id_type=MESH)

    for dz, dy in peers:
        greet(0, dz, dy)
    for p in range(1, nchan):
        for dy in range(RING):
            greet(p, 0, dy)

    loads = [pltpu.make_async_copy(src, dst, load_sem.at[n]) for n, (src, dst) in enumerate((
        (k_hbm, k_ref), (v_hbm, v_ref), (c_hbm, c_ref), (q_hbm, q_ref), (taps_hbm, taps_ref)))]
    for load in loads:
        load.start()

    row = lax.broadcasted_iota(jnp.int32, (128, 128), 0)
    lane = lax.broadcasted_iota(jnp.int32, (128, 128), 1)
    order = (lane == NFILT * (row % SHARE) + row // SHARE).astype(BF16)

    for load in loads:
        load.wait()
    for f in range(NFILT):
        ts[f] = taps_ref[f:f + 1, :].astype(F32)
    for g in range(PLANES):
        at = slice(g * 128, (g + 1) * 128)
        gated = (k_ref[:, at].astype(F32) * v_ref[:, at].astype(F32)).astype(BF16)
        sg[at, :] = dot(order, gated, 1, 1).astype(BF16)
        back = (c_ref[:, at].astype(F32) * q_ref[:, at].astype(F32)).astype(BF16)
        sb[at, :] = dot(order, back, 1, 1).astype(BF16)

    pl.semaphore_wait(barrier, CTX - 1 + (nchan - 1) * RING)

    def chunk(i):
        return pl.ds(pl.multiple_of(i * SHARE, SHARE), SHARE)

    def place(i):
        return (pl.ds(pl.multiple_of(lax.div(i, 2) * SHARE, SHARE), SHARE),
                pl.ds(pl.multiple_of(lax.rem(i, 2) * 128, 128), 128))

    my_rows, my_lanes = place(me)
    places = {(dz, dy): place(zs[dz] * RING + ys[dy]) for dz, dy in peers}

    def copy(src, dst, n, recv, p, dz, dy):
        return pltpu.make_async_remote_copy(
            src_ref=src, dst_ref=dst, send_sem=send_sem.at[n], recv_sem=recv,
            device_id=(ps[p], zs[dz] * RING + ys[dy]), device_id_type=MESH)

    def arrived(like, recv):
        copy(like, like, 0, recv, 0, 1, 0).wait_recv()

    def sent(like, n):
        copy(like, like, n, t_rs.at[0], 0, 1, 0).wait_send()

    def send_in(send, recv, n, rs):
        for dz, dy in peers:
            copy(send.at[chunk(zs[dz] * RING + ys[dy]), :], recv.at[my_rows, my_lanes], n, rs.at[0], 0, dz, dy).start()

    def send_out(send, recv, n, rs):
        for dz, dy in peers:
            r, l = places[dz, dy]
            copy(send.at[r, l], recv.at[chunk(me), :], n, rs.at[(PLANES - dz) % PLANES], 0, dz, dy).start()

    others = pl.ds(0, (CTX - 1) * SHARE)
    send_in(sg, rg, 1, g_rs)
    for dz, dy in peers:
        copy(ts.at[pl.ds(ys[dy], 1)], tr.at[pl.ds(me, 1)], 0, t_rs.at[0], 0, dz, dy).start()
    send_in(sb, rb, 2, b_rs)

    pad = GROUPS * SHARE
    tr[pl.ds(me, 1)] = ts[pl.ds(y, 1)]
    rg[my_rows, my_lanes] = sg[chunk(me), :]
    rb[my_rows, my_lanes] = sb[chunk(me), :]
    rb[NBLOCK * SHARE:NBLOCK * SHARE + pad, :] = jnp.zeros((pad, BLOCK), BF16)

    arrived(tr.at[pl.ds(0, CTX - 1)], t_rs.at[0])
    toep[0, 128:256, 0:128] = jnp.zeros((128, 128), BF16)

    def lag_block(e, this, last):
        picked = jnp.where(row + lane < 128, jnp.broadcast_to(this, (128, 128)), jnp.broadcast_to(last, (128, 128)))
        return pltpu.roll(picked, 0, 1, stride=1, stride_axis=0).astype(BF16)

    def build(d, carry):
        low = lax.max(2 * d - 1, 0)
        even = lag_block(2 * d, tr[2 * d], tr[low] * (d > 0).astype(F32))
        odd = lag_block(2 * d + 1, tr[2 * d + 1], tr[2 * d])
        toep[d, 0:128, 0:128] = even
        toep[d, 128:256, 128:256] = even
        toep[d, 0:128, 128:256] = odd
        toep[d + 1, 128:256, 0:128] = odd
        return carry

    lax.fori_loop(0, NBLOCK, build, 0)

    full = NBLOCK * SHARE
    arrived(sg.at[others], g_rs.at[0])
    for d in range(NBLOCK):
        part = dot(rg[0:full - SHARE * d, :], toep[d], 1, 0)
        if d == 0:
            acc[...] = part
        else:
            acc[SHARE * d:full, :] += part
    om[...] = acc[...].astype(BF16)
    send_out(om, bm, 3, m_rs)
    bm[chunk(me), :] = om[my_rows, my_lanes]

    sub = lax.broadcasted_iota(jnp.int32, (BLOCK, BLOCK), 0)
    col = lax.broadcasted_iota(jnp.int32, (BLOCK, BLOCK), 1)
    flip = (sub + col == BLOCK - 1).astype(BF16)
    gt_t[...] = dot(flip, rg[...], 1, 1).astype(BF16)
    arrived(sb.at[others], b_rs.at[0])
    for group in range(NBLOCK // GROUPS):
        depth = full - group * GROUPS * SHARE
        for s in range(GROUPS):
            d = group * GROUPS + s
            prod[d] = dot(gt_t[:, 0:depth], rb[SHARE * d:SHARE * d + depth, :], 1, 0)
    prod[NBLOCK] = jnp.zeros((BLOCK, BLOCK), F32)

    def lag_sums(d, carry):
        even = prod[d, 128:256, 0:128] + prod[d, 0:128, 128:256]
        odd = prod[d, 128:256, 128:256] + prod[d + 1, 0:128, 0:128]
        after = prod[d + 1, 128:256, 0:128] + prod[d + 1, 0:128, 128:256]
        for e, (this, later) in enumerate(((even, odd), (odd, after))):
            both = jnp.where(row + lane >= 127, this, later)
            fa[2 * d + e] = jnp.sum(pltpu.roll(both, 1, 1, stride=1, stride_axis=0), axis=0, keepdims=True)
        return carry

    lax.fori_loop(0, NBLOCK, lag_sums, 0)

    for dz in planes[:-1]:
        copy(fa.at[pl.ds(RING * zs[dz], RING)], ra.at[z], 5, a_rs.at[0], 0, dz, 0).start()
    ra[z] = fa[pl.ds(RING * z, RING)]

    for d in range(NBLOCK):
        part = dot(rb[SHARE * d:full, :], toep[d], 1, 1)
        if d == 0:
            acc[...] = part
        else:
            acc[0:full - SHARE * d, :] += part
    og[...] = acc[...].astype(BF16)
    send_out(og, bg, 4, o_rs)
    bg[chunk(me), :] = og[my_rows, my_lanes]

    def tiles(recv, rs, fn):
        for dz in planes:
            arrived(recv.at[pl.ds(0, (RING - (dz == 0)) * SHARE), :], rs.at[dz])
            rows = pl.ds(pl.multiple_of(zs[dz] * 128, 128), 128)
            fn(dot(recv[rows, :], order, 0, 0), rows)

    def finish_mixed(mixed, at):
        out_ref[:, at] = (q_ref[:, at].astype(F32) * mixed).astype(BF16)
        qg_ref[:, at] = (c_ref[:, at].astype(F32) * mixed).astype(BF16)

    def finish_grad(grad, at):
        kg_ref[:, at] = (grad * v_ref[:, at].astype(F32)).astype(BF16)
        vg_ref[:, at] = (grad * k_ref[:, at].astype(F32)).astype(BF16)

    arrived(fa.at[pl.ds(0, (PLANES - 1) * RING)], a_rs.at[0])
    total = ra[0]
    for p in range(1, PLANES):
        total = total + ra[p]
    sbuf[...] = total
    for p, dy in near:
        copy(sbuf.at[pl.ds(ys[dy], 1)], rf.at[pl.ds(ch * RING + y, 1)], 6, f_rs.at[0], p, 0, dy).start()
    rf[pl.ds(ch * RING + y, 1)] = sbuf[pl.ds(y, 1)]

    tiles(bm, m_rs, finish_mixed)
    tiles(bg, o_rs, finish_grad)

    arrived(rf.at[pl.ds(0, nchan * RING - 1)], f_rs.at[0])
    for f in range(NFILT):
        total = rf[f]
        for p in range(1, nchan):
            total = total + rf[p * RING + f]
        fg_ref[f:f + 1, :] = total * scale

    sent(tr.at[pl.ds(0, CTX - 1)], 0)
    for n in range(1, 5):
        sent(sg.at[others], n)
    sent(fa.at[pl.ds(0, (PLANES - 1) * RING)], 5)
    sent(rf.at[pl.ds(0, nchan * RING - 1)], 6)


def store(*refs):
    sems = refs[10]
    copies = [pltpu.make_async_copy(refs[n], refs[5 + n], sems.at[n]) for n in range(5)]
    for item in copies:
        item.start()
    for item in copies:
        item.wait()


def shards(nchan, queries, keys, values, filters, cotangent):
    rows, width = queries.shape
    tokens = rows * CTX
    scale = (tokens * (nchan * width // NFILT)) ** (-0.5)
    vmem = pl.BlockSpec(memory_space=pltpu.VMEM)
    dma = pltpu.SemaphoreType.DMA
    full = NBLOCK * SHARE
    act = jax.ShapeDtypeStruct((rows, width), BF16)
    queries, keys, values, filters, cotangent = [pltpu.with_memory_space_constraint(x, pltpu.HBM) for x in (queries, keys, values, filters, cotangent)]
    held = pl.pallas_call(
        functools.partial(kernel, nchan, scale),
        out_shape=(act, act, act, act, jax.ShapeDtypeStruct((NFILT, rows), F32)),
        in_specs=[pl.BlockSpec(memory_space=pltpu.HBM)] * 5,
        out_specs=[vmem] * 5,
        scratch_shapes=[
            pltpu.VMEM((rows, width), BF16),
            pltpu.VMEM((rows, width), BF16),
            pltpu.VMEM((rows, width), BF16),
            pltpu.VMEM((NFILT, rows), BF16),
            pltpu.VMEM((rows, width), BF16),
            dma((5,)),
            pltpu.VMEM((width, rows), BF16),
            pltpu.VMEM((width, rows), BF16),
            pltpu.VMEM((full, BLOCK), BF16),
            pltpu.VMEM((full + GROUPS * SHARE, BLOCK), BF16),
            pltpu.VMEM((full, BLOCK), BF16),
            pltpu.VMEM((full, BLOCK), BF16),
            pltpu.VMEM((width, rows), BF16),
            pltpu.VMEM((width, rows), BF16),
            pltpu.VMEM((NFILT, 1, rows), F32),
            pltpu.VMEM((CTX, 1, rows), F32),
            pltpu.VMEM((NBLOCK + 1, BLOCK, BLOCK), BF16),
            pltpu.VMEM((full, BLOCK), F32),
            pltpu.VMEM((BLOCK, full), BF16),
            pltpu.VMEM((NBLOCK + 1, BLOCK, BLOCK), F32),
            pltpu.VMEM((CTX, 1, rows), F32),
            pltpu.VMEM((PLANES, RING, 1, rows), F32),
            pltpu.VMEM((RING, 1, rows), F32),
            pltpu.VMEM((nchan * RING, 1, rows), F32),
        ] + [dma((7,))] + [dma((1,))] * 3 + [dma((PLANES,))] * 2 + [dma((1,))] * 2,
        compiler_params=pltpu.CompilerParams(
            collective_id=0, has_side_effects=True, vmem_limit_bytes=40000000
        ),
    )(queries, keys, values, filters, cotangent)
    return pl.pallas_call(
        store,
        out_shape=(act, act, act, act, jax.ShapeDtypeStruct((NFILT, rows), F32)),
        in_specs=[vmem] * 5,
        out_specs=[pl.BlockSpec(memory_space=pltpu.HBM)] * 5,
        scratch_shapes=[dma((5,))],
        compiler_params=pltpu.CompilerParams(vmem_limit_bytes=4 * 1024 * 1024),
    )(*held)


def solution(mesh):
    act = P("ctx", "chan")
    taps = P(None, "ctx")
    return jax.shard_map(
        functools.partial(shards, mesh.shape["chan"]),
        mesh=mesh,
        in_specs=(act, act, act, taps, act),
        out_specs=(act, act, act, act, taps),
        check_vma=False,
    )
```

```python
import functools

import jax
import jax.numpy as jnp
from jax import lax
from jax.experimental import pallas as pl
from jax.experimental.pallas import tpu as pltpu
from jax.sharding import PartitionSpec as P

NFILT = 4
PLANES = 8
RING = 4
CTX = PLANES * RING
ROWS = 128
BLOCK = 256
NBLOCK = 16
SHARE = 32
GROUPS = 4
MESH = pl.DeviceIdType.MESH
F32 = jnp.float32
BF16 = jnp.bfloat16


def dot(a, b, ca, cb):
    return lax.dot_general(a, b, (((ca,), (cb,)), ((), ())), preferred_element_type=F32)


def kernel(nchan, scale,
           q_hbm, k_hbm, v_hbm, taps_hbm, c_hbm,
           out_ref, qg_ref, kg_ref, vg_ref, fg_ref,
           q_ref, k_ref, v_ref, taps_ref, c_ref, load_sem,
           sg, sb, rg, rb, om, og, bm, bg, ts, tr, toep, acc, gt_t, prod, fold, fa, ra, sbuf, rf,
           send_sem, t_rs, g_rs, b_rs, m_rs, o_rs, a_rs, f_rs):
    ch = lax.axis_index("chan")
    me = lax.axis_index("ctx")
    z = lax.div(me, RING)
    y = lax.rem(me, RING)
    zs = [z] + [lax.rem(z + dz, PLANES) for dz in range(1, PLANES)]
    ys = [y] + [lax.rem(y + dy, RING) for dy in range(1, RING)]
    ps = [ch] + [lax.rem(ch + p, nchan) for p in range(1, nchan)]
    planes = (4, 3, 5, 2, 6, 1, 7, 0)
    peers = [(dz, dy) for dz in planes for dy in range(RING) if dz or dy]
    near = [(p, dy) for p in range(nchan) for dy in range(RING) if p or dy]

    barrier = pltpu.get_barrier_semaphore()

    def greet(p, dz, dy):
        pl.semaphore_signal(barrier, inc=1, device_id=(ps[p], zs[dz] * RING + ys[dy]), device_id_type=MESH)

    for dz, dy in peers:
        greet(0, dz, dy)
    for p in range(1, nchan):
        for dy in range(RING):
            greet(p, 0, dy)

    loads = [pltpu.make_async_copy(src, dst, load_sem.at[n]) for n, (src, dst) in enumerate((
        (k_hbm, k_ref), (v_hbm, v_ref), (c_hbm, c_ref), (q_hbm, q_ref), (taps_hbm, taps_ref)))]
    for load in loads:
        load.start()

    row = lax.broadcasted_iota(jnp.int32, (128, 128), 0)
    lane = lax.broadcasted_iota(jnp.int32, (128, 128), 1)
    order = (lane == NFILT * (row % SHARE) + row // SHARE).astype(BF16)

    for load in loads:
        load.wait()
    for f in range(NFILT):
        ts[f] = taps_ref[f:f + 1, :].astype(F32)
    for g in range(PLANES):
        at = slice(g * 128, (g + 1) * 128)
        gated = (k_ref[:, at].astype(F32) * v_ref[:, at].astype(F32)).astype(BF16)
        sg[at, :] = dot(order, gated, 1, 1).astype(BF16)
        back = (c_ref[:, at].astype(F32) * q_ref[:, at].astype(F32)).astype(BF16)
        sb[at, :] = dot(order, back, 1, 1).astype(BF16)

    pl.semaphore_wait(barrier, CTX - 1 + (nchan - 1) * RING)

    def chunk(i):
        return pl.ds(pl.multiple_of(i * SHARE, SHARE), SHARE)

    def place(i):
        return (pl.ds(pl.multiple_of(lax.div(i, 2) * SHARE, SHARE), SHARE),
                pl.ds(pl.multiple_of(lax.rem(i, 2) * 128, 128), 128))

    my_rows, my_lanes = place(me)
    places = {(dz, dy): place(zs[dz] * RING + ys[dy]) for dz, dy in peers}

    def copy(src, dst, n, recv, p, dz, dy):
        return pltpu.make_async_remote_copy(
            src_ref=src, dst_ref=dst, send_sem=send_sem.at[n], recv_sem=recv,
            device_id=(ps[p], zs[dz] * RING + ys[dy]), device_id_type=MESH)

    def arrived(like, recv):
        copy(like, like, 0, recv, 0, 1, 0).wait_recv()

    def sent(like, n):
        copy(like, like, n, t_rs.at[0], 0, 1, 0).wait_send()

    def send_in(send, recv, n, rs):
        for dz, dy in peers:
            copy(send.at[chunk(zs[dz] * RING + ys[dy]), :], recv.at[my_rows, my_lanes], n, rs.at[0], 0, dz, dy).start()

    def send_out(send, recv, n, rs, which=peers):
        for dz, dy in which:
            r, l = places[dz, dy]
            copy(send.at[r, l], recv.at[chunk(me), :], n, rs.at[(PLANES - dz) % PLANES], 0, dz, dy).start()

    others = pl.ds(0, (CTX - 1) * SHARE)
    send_in(sg, rg, 1, g_rs)
    for dz, dy in peers:
        copy(ts.at[pl.ds(ys[dy], 1)], tr.at[pl.ds(me, 1)], 0, t_rs.at[0], 0, dz, dy).start()
    send_in(sb, rb, 2, b_rs)

    pad = GROUPS * SHARE
    tr[pl.ds(me, 1)] = ts[pl.ds(y, 1)]
    rg[my_rows, my_lanes] = sg[chunk(me), :]
    rb[my_rows, my_lanes] = sb[chunk(me), :]
    rb[NBLOCK * SHARE:NBLOCK * SHARE + pad, :] = jnp.zeros((pad, BLOCK), BF16)

    arrived(tr.at[pl.ds(0, CTX - 1)], t_rs.at[0])
    toep[0, 128:256, 0:128] = jnp.zeros((128, 128), BF16)

    def lag_block(e, this, last):
        picked = jnp.where(row + lane < 128, jnp.broadcast_to(this, (128, 128)), jnp.broadcast_to(last, (128, 128)))
        return pltpu.roll(picked, 0, 1, stride=1, stride_axis=0).astype(BF16)

    def build(d, carry):
        low = lax.max(2 * d - 1, 0)
        even = lag_block(2 * d, tr[2 * d], tr[low] * (d > 0).astype(F32))
        odd = lag_block(2 * d + 1, tr[2 * d + 1], tr[2 * d])
        toep[d, 0:128, 0:128] = even
        toep[d, 128:256, 128:256] = even
        toep[d, 0:128, 128:256] = odd
        toep[d + 1, 128:256, 0:128] = odd
        return carry

    lax.fori_loop(0, NBLOCK, build, 0)

    full = NBLOCK * SHARE
    arrived(sg.at[others], g_rs.at[0])
    for d in range(NBLOCK):
        part = dot(rg[0:full - SHARE * d, :], toep[d], 1, 0)
        if d == 0:
            acc[...] = part
        else:
            acc[SHARE * d:full, :] += part
    om[...] = acc[...].astype(BF16)
    held = planes[-3:]
    send_out(om, bm, 3, m_rs, [peer for peer in peers if peer[0] not in held])
    bm[chunk(me), :] = om[my_rows, my_lanes]

    sub = lax.broadcasted_iota(jnp.int32, (BLOCK, BLOCK), 0)
    col = lax.broadcasted_iota(jnp.int32, (BLOCK, BLOCK), 1)
    flip = (sub + col == BLOCK - 1).astype(BF16)
    gt_t[...] = dot(flip, rg[...], 1, 1).astype(BF16)
    arrived(sb.at[others], b_rs.at[0])
    def product(d):
        depth = full - d // GROUPS * GROUPS * SHARE
        prod[d] = dot(gt_t[:, 0:depth], rb[SHARE * d:SHARE * d + depth, :], 1, 0)

    def diagonals(e):
        d = e // 2
        if e % 2:
            return prod[d, 128:256, 128:256] + prod[d + 1, 0:128, 0:128]
        return prod[d, 128:256, 0:128] + prod[d, 0:128, 128:256]

    prod[NBLOCK] = jnp.zeros((BLOCK, BLOCK), F32)
    wide = row + lane >= 127
    later = jnp.zeros((128, 128), F32)
    for d in range(NBLOCK - 1, -1, -1):
        product(d)
        for e in (2 * d + 1, 2 * d):
            this = diagonals(e)
            both = pltpu.roll(jnp.where(wide, this, later), 1, 1, stride=1, stride_axis=0)
            fold[e] = jnp.sum(both.reshape(16, 8, 128), axis=0)
            later = this
    for e in range(CTX):
        fa[e] = jnp.sum(fold[e], axis=0, keepdims=True)

    for dz in planes[:-1]:
        copy(fa.at[pl.ds(RING * zs[dz], RING)], ra.at[z], 5, a_rs.at[0], 0, dz, 0).start()
    ra[z] = fa[pl.ds(RING * z, RING)]
    send_out(om, bm, 3, m_rs, [peer for peer in peers if peer[0] in held])

    for d in range(NBLOCK):
        part = dot(rb[SHARE * d:full, :], toep[d], 1, 1)
        if d == 0:
            acc[...] = part
        else:
            acc[0:full - SHARE * d, :] += part
    og[...] = acc[...].astype(BF16)
    send_out(og, bg, 4, o_rs)
    bg[chunk(me), :] = og[my_rows, my_lanes]

    def tiles(recv, rs, fn):
        for dz in planes:
            arrived(recv.at[pl.ds(0, (RING - (dz == 0)) * SHARE), :], rs.at[dz])
            rows = pl.ds(pl.multiple_of(zs[dz] * 128, 128), 128)
            fn(dot(recv[rows, :], order, 0, 0), rows)

    def finish_mixed(mixed, at):
        out_ref[:, at] = (q_ref[:, at].astype(F32) * mixed).astype(BF16)
        qg_ref[:, at] = (c_ref[:, at].astype(F32) * mixed).astype(BF16)

    def finish_grad(grad, at):
        kg_ref[:, at] = (grad * v_ref[:, at].astype(F32)).astype(BF16)
        vg_ref[:, at] = (grad * k_ref[:, at].astype(F32)).astype(BF16)

    arrived(fa.at[pl.ds(0, (PLANES - 1) * RING)], a_rs.at[0])
    total = ra[0]
    for p in range(1, PLANES):
        total = total + ra[p]
    sbuf[...] = total
    for p, dy in near:
        copy(sbuf.at[pl.ds(ys[dy], 1)], rf.at[pl.ds(ch * RING + y, 1)], 6, f_rs.at[0], p, 0, dy).start()
    rf[pl.ds(ch * RING + y, 1)] = sbuf[pl.ds(y, 1)]

    tiles(bm, m_rs, finish_mixed)
    tiles(bg, o_rs, finish_grad)

    arrived(rf.at[pl.ds(0, nchan * RING - 1)], f_rs.at[0])
    for f in range(NFILT):
        total = rf[f]
        for p in range(1, nchan):
            total = total + rf[p * RING + f]
        fg_ref[f:f + 1, :] = total * scale

    sent(tr.at[pl.ds(0, CTX - 1)], 0)
    for n in range(1, 5):
        sent(sg.at[others], n)
    sent(fa.at[pl.ds(0, (PLANES - 1) * RING)], 5)
    sent(rf.at[pl.ds(0, nchan * RING - 1)], 6)


def store(*refs):
    sems = refs[10]
    copies = [pltpu.make_async_copy(refs[n], refs[5 + n], sems.at[n]) for n in range(5)]
    for item in copies:
        item.start()
    for item in copies:
        item.wait()


def shards(nchan, queries, keys, values, filters, cotangent):
    rows, width = queries.shape
    tokens = rows * CTX
    scale = (tokens * (nchan * width // NFILT)) ** (-0.5)
    vmem = pl.BlockSpec(memory_space=pltpu.VMEM)
    dma = pltpu.SemaphoreType.DMA
    full = NBLOCK * SHARE
    act = jax.ShapeDtypeStruct((rows, width), BF16)
    queries, keys, values, filters, cotangent = [pltpu.with_memory_space_constraint(x, pltpu.HBM) for x in (queries, keys, values, filters, cotangent)]
    held = pl.pallas_call(
        functools.partial(kernel, nchan, scale),
        out_shape=(act, act, act, act, jax.ShapeDtypeStruct((NFILT, rows), F32)),
        in_specs=[pl.BlockSpec(memory_space=pltpu.HBM)] * 5,
        out_specs=[vmem] * 5,
        scratch_shapes=[
            pltpu.VMEM((rows, width), BF16),
            pltpu.VMEM((rows, width), BF16),
            pltpu.VMEM((rows, width), BF16),
            pltpu.VMEM((NFILT, rows), BF16),
            pltpu.VMEM((rows, width), BF16),
            dma((5,)),
            pltpu.VMEM((width, rows), BF16),
            pltpu.VMEM((width, rows), BF16),
            pltpu.VMEM((full, BLOCK), BF16),
            pltpu.VMEM((full + GROUPS * SHARE, BLOCK), BF16),
            pltpu.VMEM((full, BLOCK), BF16),
            pltpu.VMEM((full, BLOCK), BF16),
            pltpu.VMEM((width, rows), BF16),
            pltpu.VMEM((width, rows), BF16),
            pltpu.VMEM((NFILT, 1, rows), F32),
            pltpu.VMEM((CTX, 1, rows), F32),
            pltpu.VMEM((NBLOCK + 1, BLOCK, BLOCK), BF16),
            pltpu.VMEM((full, BLOCK), F32),
            pltpu.VMEM((BLOCK, full), BF16),
            pltpu.VMEM((NBLOCK + 1, BLOCK, BLOCK), F32),
            pltpu.VMEM((CTX, 8, rows), F32),
            pltpu.VMEM((CTX, 1, rows), F32),
            pltpu.VMEM((PLANES, RING, 1, rows), F32),
            pltpu.VMEM((RING, 1, rows), F32),
            pltpu.VMEM((nchan * RING, 1, rows), F32),
        ] + [dma((7,))] + [dma((1,))] * 3 + [dma((PLANES,))] * 2 + [dma((1,))] * 2,
        compiler_params=pltpu.CompilerParams(
            collective_id=0, has_side_effects=True, vmem_limit_bytes=40000000
        ),
    )(queries, keys, values, filters, cotangent)
    return pl.pallas_call(
        store,
        out_shape=(act, act, act, act, jax.ShapeDtypeStruct((NFILT, rows), F32)),
        in_specs=[vmem] * 5,
        out_specs=[pl.BlockSpec(memory_space=pltpu.HBM)] * 5,
        scratch_shapes=[dma((5,))],
        compiler_params=pltpu.CompilerParams(vmem_limit_bytes=4 * 1024 * 1024),
    )(*held)


def solution(mesh):
    act = P("ctx", "chan")
    taps = P(None, "ctx")
    return jax.shard_map(
        functools.partial(shards, mesh.shape["chan"]),
        mesh=mesh,
        in_specs=(act, act, act, taps, act),
        out_specs=(act, act, act, act, taps),
        check_vma=False,
    )
```

```python
import functools

import jax
import jax.numpy as jnp
from jax import lax
from jax.experimental import pallas as pl
from jax.experimental.pallas import tpu as pltpu
from jax.sharding import PartitionSpec as P

NFILT = 4
PLANES = 8
RING = 4
CTX = PLANES * RING
ROWS = 128
BLOCK = 256
NBLOCK = 16
SHARE = 32
GROUPS = 4
MESH = pl.DeviceIdType.MESH
F32 = jnp.float32
BF16 = jnp.bfloat16


def dot(a, b, ca, cb):
    return lax.dot_general(a, b, (((ca,), (cb,)), ((), ())), preferred_element_type=F32)


def kernel(nchan, scale,
           q_hbm, k_hbm, v_hbm, taps_hbm, c_hbm,
           out_ref, qg_ref, kg_ref, vg_ref, fg_ref,
           q_ref, k_ref, v_ref, taps_ref, c_ref, load_sem,
           sg, sb, rg, rb, om, og, bm, bg, ts, tr, toep, acc, gt_t, prod, fold, fa, ra, sbuf, rf,
           send_sem, t_rs, g_rs, b_rs, m_rs, o_rs, a_rs, f_rs):
    ch = lax.axis_index("chan")
    me = lax.axis_index("ctx")
    z = lax.div(me, RING)
    y = lax.rem(me, RING)
    zs = [z] + [lax.rem(z + dz, PLANES) for dz in range(1, PLANES)]
    ys = [y] + [lax.rem(y + dy, RING) for dy in range(1, RING)]
    ps = [ch] + [lax.rem(ch + p, nchan) for p in range(1, nchan)]
    planes = (4, 3, 5, 2, 6, 1, 7, 0)
    peers = [(dz, dy) for dz in planes for dy in range(RING) if dz or dy]
    far = sorted(range(nchan), key=lambda p: -min(p, nchan - p))
    near = [(p, dy) for p in far for dy in (2, 1, 3, 0) if p or dy]

    barrier = pltpu.get_barrier_semaphore()

    def greet(p, dz, dy):
        pl.semaphore_signal(barrier, inc=1, device_id=(ps[p], zs[dz] * RING + ys[dy]), device_id_type=MESH)

    for dz, dy in peers:
        greet(0, dz, dy)
    for p in range(1, nchan):
        for dy in range(RING):
            greet(p, 0, dy)

    loads = [pltpu.make_async_copy(src, dst, load_sem.at[n]) for n, (src, dst) in enumerate((
        (k_hbm, k_ref), (v_hbm, v_ref), (c_hbm, c_ref), (q_hbm, q_ref), (taps_hbm, taps_ref)))]
    for load in loads:
        load.start()

    row = lax.broadcasted_iota(jnp.int32, (128, 128), 0)
    lane = lax.broadcasted_iota(jnp.int32, (128, 128), 1)
    order = (lane == NFILT * (row % SHARE) + row // SHARE).astype(BF16)

    for load in loads:
        load.wait()
    for f in range(NFILT):
        ts[f] = taps_ref[f:f + 1, :].astype(F32)
    for g in range(PLANES):
        at = slice(g * 128, (g + 1) * 128)
        gated = (k_ref[:, at].astype(F32) * v_ref[:, at].astype(F32)).astype(BF16)
        sg[at, :] = dot(order, gated, 1, 1).astype(BF16)
        back = (c_ref[:, at].astype(F32) * q_ref[:, at].astype(F32)).astype(BF16)
        sb[at, :] = dot(order, back, 1, 1).astype(BF16)

    pl.semaphore_wait(barrier, CTX - 1 + (nchan - 1) * RING)

    def chunk(i):
        return pl.ds(pl.multiple_of(i * SHARE, SHARE), SHARE)

    def place(i):
        return (pl.ds(pl.multiple_of(lax.div(i, 2) * SHARE, SHARE), SHARE),
                pl.ds(pl.multiple_of(lax.rem(i, 2) * 128, 128), 128))

    my_rows, my_lanes = place(me)
    places = {(dz, dy): place(zs[dz] * RING + ys[dy]) for dz, dy in peers}

    def copy(src, dst, n, recv, p, dz, dy):
        return pltpu.make_async_remote_copy(
            src_ref=src, dst_ref=dst, send_sem=send_sem.at[n], recv_sem=recv,
            device_id=(ps[p], zs[dz] * RING + ys[dy]), device_id_type=MESH)

    def arrived(like, recv):
        copy(like, like, 0, recv, 0, 1, 0).wait_recv()

    def sent(like, n):
        copy(like, like, n, t_rs.at[0], 0, 1, 0).wait_send()

    def send_in(send, recv, n, rs):
        for dz, dy in peers:
            copy(send.at[chunk(zs[dz] * RING + ys[dy]), :], recv.at[my_rows, my_lanes], n, rs.at[0], 0, dz, dy).start()

    def send_out(send, recv, n, rs, which=peers):
        for dz, dy in which:
            r, l = places[dz, dy]
            copy(send.at[r, l], recv.at[chunk(me), :], n, rs.at[(PLANES - dz) % PLANES], 0, dz, dy).start()

    others = pl.ds(0, (CTX - 1) * SHARE)
    send_in(sg, rg, 1, g_rs)
    for dz, dy in peers:
        copy(ts.at[pl.ds(ys[dy], 1)], tr.at[pl.ds(me, 1)], 0, t_rs.at[0], 0, dz, dy).start()
    send_in(sb, rb, 2, b_rs)

    pad = GROUPS * SHARE
    tr[pl.ds(me, 1)] = ts[pl.ds(y, 1)]
    rg[my_rows, my_lanes] = sg[chunk(me), :]
    rb[my_rows, my_lanes] = sb[chunk(me), :]
    rb[NBLOCK * SHARE:NBLOCK * SHARE + pad, :] = jnp.zeros((pad, BLOCK), BF16)

    arrived(tr.at[pl.ds(0, CTX - 1)], t_rs.at[0])
    toep[0, 128:256, 0:128] = jnp.zeros((128, 128), BF16)

    def lag_block(e, this, last):
        picked = jnp.where(row + lane < 128, jnp.broadcast_to(this, (128, 128)), jnp.broadcast_to(last, (128, 128)))
        return pltpu.roll(picked, 0, 1, stride=1, stride_axis=0).astype(BF16)

    def build(d, carry):
        low = lax.max(2 * d - 1, 0)
        even = lag_block(2 * d, tr[2 * d], tr[low] * (d > 0).astype(F32))
        odd = lag_block(2 * d + 1, tr[2 * d + 1], tr[2 * d])
        toep[d, 0:128, 0:128] = even
        toep[d, 128:256, 128:256] = even
        toep[d, 0:128, 128:256] = odd
        toep[d + 1, 128:256, 0:128] = odd
        return carry

    lax.fori_loop(0, NBLOCK, build, 0)

    full = NBLOCK * SHARE
    arrived(sg.at[others], g_rs.at[0])
    for d in range(NBLOCK):
        part = dot(rg[0:full - SHARE * d, :], toep[d], 1, 0)
        if d == 0:
            acc[...] = part
        else:
            acc[SHARE * d:full, :] += part
    om[...] = acc[...].astype(BF16)
    held = planes[-3:]
    send_out(om, bm, 3, m_rs, [peer for peer in peers if peer[0] not in held])
    bm[chunk(me), :] = om[my_rows, my_lanes]

    sub = lax.broadcasted_iota(jnp.int32, (BLOCK, BLOCK), 0)
    col = lax.broadcasted_iota(jnp.int32, (BLOCK, BLOCK), 1)
    flip = (sub + col == BLOCK - 1).astype(BF16)
    gt_t[...] = dot(flip, rg[...], 1, 1).astype(BF16)
    arrived(sb.at[others], b_rs.at[0])
    def product(d):
        depth = full - d // GROUPS * GROUPS * SHARE
        prod[d] = dot(gt_t[:, 0:depth], rb[SHARE * d:SHARE * d + depth, :], 1, 0)

    def diagonals(e):
        d = e // 2
        if e % 2:
            return prod[d, 128:256, 128:256] + prod[d + 1, 0:128, 0:128]
        return prod[d, 128:256, 0:128] + prod[d, 0:128, 128:256]

    prod[NBLOCK] = jnp.zeros((BLOCK, BLOCK), F32)
    wide = row + lane >= 127
    later = jnp.zeros((128, 128), F32)
    for d in range(NBLOCK - 1, -1, -1):
        product(d)
        for e in (2 * d + 1, 2 * d):
            this = diagonals(e)
            both = pltpu.roll(jnp.where(wide, this, later), 1, 1, stride=1, stride_axis=0)
            fold[e] = jnp.sum(both.reshape(16, 8, 128), axis=0)
            later = this
    for e in range(CTX):
        fa[e] = jnp.sum(fold[e], axis=0, keepdims=True)

    for dz in planes[:-1]:
        copy(fa.at[pl.ds(RING * zs[dz], RING)], ra.at[z], 5, a_rs.at[0], 0, dz, 0).start()
    ra[z] = fa[pl.ds(RING * z, RING)]
    send_out(om, bm, 3, m_rs, [peer for peer in peers if peer[0] in held])

    for d in range(NBLOCK):
        part = dot(rb[SHARE * d:full, :], toep[d], 1, 1)
        if d == 0:
            acc[...] = part
        else:
            acc[0:full - SHARE * d, :] += part
    og[...] = acc[...].astype(BF16)
    kept = planes[-2:]
    send_out(og, bg, 4, o_rs, [peer for peer in peers if peer[0] not in kept])
    bg[chunk(me), :] = og[my_rows, my_lanes]

    def tiles(recv, rs, fn):
        for dz in planes:
            arrived(recv.at[pl.ds(0, (RING - (dz == 0)) * SHARE), :], rs.at[dz])
            rows = pl.ds(pl.multiple_of(zs[dz] * 128, 128), 128)
            fn(dot(recv[rows, :], order, 0, 0), rows)

    def finish_mixed(mixed, at):
        out_ref[:, at] = (q_ref[:, at].astype(F32) * mixed).astype(BF16)
        qg_ref[:, at] = (c_ref[:, at].astype(F32) * mixed).astype(BF16)

    def finish_grad(grad, at):
        kg_ref[:, at] = (grad * v_ref[:, at].astype(F32)).astype(BF16)
        vg_ref[:, at] = (grad * k_ref[:, at].astype(F32)).astype(BF16)

    arrived(fa.at[pl.ds(0, (PLANES - 1) * RING)], a_rs.at[0])
    total = ra[0]
    for p in range(1, PLANES):
        total = total + ra[p]
    sbuf[...] = total
    for p, dy in near:
        copy(sbuf.at[pl.ds(ys[dy], 1)], rf.at[pl.ds(ch * RING + y, 1)], 6, f_rs.at[0], p, 0, dy).start()
    rf[pl.ds(ch * RING + y, 1)] = sbuf[pl.ds(y, 1)]

    send_out(og, bg, 4, o_rs, [peer for peer in peers if peer[0] in kept])
    tiles(bm, m_rs, finish_mixed)
    tiles(bg, o_rs, finish_grad)

    arrived(rf.at[pl.ds(0, nchan * RING - 1)], f_rs.at[0])
    for f in range(NFILT):
        total = rf[f]
        for p in range(1, nchan):
            total = total + rf[p * RING + f]
        fg_ref[f:f + 1, :] = total * scale

    sent(tr.at[pl.ds(0, CTX - 1)], 0)
    for n in range(1, 5):
        sent(sg.at[others], n)
    sent(fa.at[pl.ds(0, (PLANES - 1) * RING)], 5)
    sent(rf.at[pl.ds(0, nchan * RING - 1)], 6)


def store(*refs):
    sems = refs[10]
    copies = [pltpu.make_async_copy(refs[n], refs[5 + n], sems.at[n]) for n in range(5)]
    for item in copies:
        item.start()
    for item in copies:
        item.wait()


def shards(nchan, queries, keys, values, filters, cotangent):
    rows, width = queries.shape
    tokens = rows * CTX
    scale = (tokens * (nchan * width // NFILT)) ** (-0.5)
    vmem = pl.BlockSpec(memory_space=pltpu.VMEM)
    dma = pltpu.SemaphoreType.DMA
    full = NBLOCK * SHARE
    act = jax.ShapeDtypeStruct((rows, width), BF16)
    queries, keys, values, filters, cotangent = [pltpu.with_memory_space_constraint(x, pltpu.HBM) for x in (queries, keys, values, filters, cotangent)]
    held = pl.pallas_call(
        functools.partial(kernel, nchan, scale),
        out_shape=(act, act, act, act, jax.ShapeDtypeStruct((NFILT, rows), F32)),
        in_specs=[pl.BlockSpec(memory_space=pltpu.HBM)] * 5,
        out_specs=[vmem] * 5,
        scratch_shapes=[
            pltpu.VMEM((rows, width), BF16),
            pltpu.VMEM((rows, width), BF16),
            pltpu.VMEM((rows, width), BF16),
            pltpu.VMEM((NFILT, rows), BF16),
            pltpu.VMEM((rows, width), BF16),
            dma((5,)),
            pltpu.VMEM((width, rows), BF16),
            pltpu.VMEM((width, rows), BF16),
            pltpu.VMEM((full, BLOCK), BF16),
            pltpu.VMEM((full + GROUPS * SHARE, BLOCK), BF16),
            pltpu.VMEM((full, BLOCK), BF16),
            pltpu.VMEM((full, BLOCK), BF16),
            pltpu.VMEM((width, rows), BF16),
            pltpu.VMEM((width, rows), BF16),
            pltpu.VMEM((NFILT, 1, rows), F32),
            pltpu.VMEM((CTX, 1, rows), F32),
            pltpu.VMEM((NBLOCK + 1, BLOCK, BLOCK), BF16),
            pltpu.VMEM((full, BLOCK), F32),
            pltpu.VMEM((BLOCK, full), BF16),
            pltpu.VMEM((NBLOCK + 1, BLOCK, BLOCK), F32),
            pltpu.VMEM((CTX, 8, rows), F32),
            pltpu.VMEM((CTX, 1, rows), F32),
            pltpu.VMEM((PLANES, RING, 1, rows), F32),
            pltpu.VMEM((RING, 1, rows), F32),
            pltpu.VMEM((nchan * RING, 1, rows), F32),
        ] + [dma((7,))] + [dma((1,))] * 3 + [dma((PLANES,))] * 2 + [dma((1,))] * 2,
        compiler_params=pltpu.CompilerParams(
            collective_id=0, has_side_effects=True, vmem_limit_bytes=40000000
        ),
    )(queries, keys, values, filters, cotangent)
    return pl.pallas_call(
        store,
        out_shape=(act, act, act, act, jax.ShapeDtypeStruct((NFILT, rows), F32)),
        in_specs=[vmem] * 5,
        out_specs=[pl.BlockSpec(memory_space=pltpu.HBM)] * 5,
        scratch_shapes=[dma((5,))],
        compiler_params=pltpu.CompilerParams(vmem_limit_bytes=4 * 1024 * 1024),
    )(*held)


def solution(mesh):
    act = P("ctx", "chan")
    taps = P(None, "ctx")
    return jax.shard_map(
        functools.partial(shards, mesh.shape["chan"]),
        mesh=mesh,
        in_specs=(act, act, act, taps, act),
        out_specs=(act, act, act, act, taps),
        check_vma=False,
    )
```
